32 devices in a mesh: group: 2 (over y), expert: 16 (over z, x, core).
Axes of the slice: x: 2, y: 2, z: 4, core: 2. Of those that a mesh axis runs over, the one named last changes fastest.
Arguments:
- tokens: bfloat16 [256, 7168], P(('group', 'expert')), parts along dimension 0, may hold values from -6 to 6
- expert_ids: int32 [256, 8], P(('group', 'expert')), parts along dimension 0, may hold values from 0 to 15, all different within a row; in each aligned block of 8 rows (0 to 7, 8 to 15, ...) at most 5 rows name the same one
- gate_probs: float32 [256, 8], P(('group', 'expert')), parts along dimension 0, may hold values from 0.05 to 0.6
- gate_proj: bfloat16 [7168, 32768], P(None, 'expert'), may hold values from -0.0625 to 0.0625
- up_proj: bfloat16 [7168, 32768], P(None, 'expert'), may hold values from -0.0625 to 0.0625
- down_proj: bfloat16 [32768, 7168], P('expert'), may hold values from -0.125 to 0.125
Outputs:
- mixed: bfloat16 [256, 7168], P(('group', 'expert')), parts along dimension 0
The draws below stay inside these ranges and needn't reach their ends.
There are 2 independent parts, one for each index of `group`. The reference program is written for one: setup_inputs(seed, part) draws one part's arguments, and reference() takes and returns one part's arrays. A program takes and returns all parts, laid end to end along the dimension named above; an argument that names none is the same for every part. Nothing has to cross between parts.
Inputs may be any that keep to these rules, and one draw needn't show every extreme that they name: `expert_ids`: each row names 8 different experts. Among the 8 tokens of one device (aligned blocks of 8 rows) no expert is named by more than 5 tokens, a bound that some blocks reach.
All inputs are finite; a program needn't handle non-finite values.
Results may differ from the reference program's by a relative error of at most 0.0051.
Values may be sent and summed in bfloat16 or wider, within the bound.
No kernel may reach another device: no remote copies, remote signals or barrier semaphores. Data moves between devices by JAX's collectives and lax.ppermute only.
A program may use at most 192 MiB of HBM per device.

```python
import math
import jax
import jax.numpy as jnp
import numpy as np
from jax import lax

D = 7168
FF = 2048
EXPERTS = 16
TOP = 8
TOK_DEV = 8
CAP = 5
TOKENS = 128
N_EXPERT = 16


def block_scale(stream_key, shape, cuts, low, top_value):
    loudness, own = 1.0, jax.random.fold_in(stream_key, 6)
    for axis_at, parts in cuts:
        draws = jnp.exp(jax.random.uniform(jax.random.fold_in(own, axis_at), (parts,), jnp.float32, low / len(cuts), top_value / len(cuts)))
        loudness = loudness * jnp.repeat(draws, shape[axis_at] // parts).reshape([-1 if axis == axis_at else 1 for axis in range(len(shape))])
    return loudness


def routed_block(own_key, own, number, rows, number_of, top, bound, skew):
    order = jax.random.permutation(own_key, number_of)
    heavy_load, ordinary = load_shares(number_of, rows * top, bound, skew, True), load_shares(number_of, rows * top, bound, skew, False)
    places = jnp.arange(number_of)

    def named(lengths, rotation):
        used = int((lengths > 0).sum())
        fixed = max(1, used // 4)
        moved = fixed + (places - fixed + rotation * (used - fixed)) % max(1, number_of - fixed)
        return jnp.zeros((number_of,), jnp.int32).at[order[jnp.where(places < fixed, places, moved)]].set(jnp.asarray(lengths, jnp.int32))

    lengths = jnp.where(number % 4 == 0, named(heavy_load, number // 4), named(ordinary, number - number // 4 - 1))
    mixed = jax.random.permutation(jax.random.fold_in(own, 3), number_of)
    source_of, receiver = mixed[0:number_of // 2 * 2:2], mixed[1:number_of // 2 * 2:2]
    slack = jnp.minimum(lengths[source_of] - 1, bound - lengths[receiver]) // 2
    slack = jnp.where((source_of == order[0]) | (receiver == order[0]) | (lengths[receiver] == 0), 0, jnp.maximum(slack, 0))
    moved = jax.random.randint(jax.random.fold_in(own, 4), (number_of // 2,), 0, 1 << 20) % (slack + 1)
    lengths = lengths.at[source_of].add(-moved).at[receiver].add(moved)
    labels = jnp.searchsorted(jnp.cumsum(lengths), jnp.arange(rows * top), side="right").astype(jnp.int32)
    grid = labels.reshape(top, rows).T
    grid = grid[jax.random.permutation(jax.random.fold_in(own, 1), rows)]
    rotation = jax.random.randint(jax.random.fold_in(own, 2), (rows, 1), 0, top)
    return jnp.take_along_axis(grid, (jnp.arange(top)[None, :] + rotation) % top, axis=1)


def load_shares(count, total, most, skew, full):
    weights = [(1 << 20) // math.isqrt(grade ** skew) + 1 for grade in range(1, count + 1)]
    largest = most if full else min(most, max(-(-total // count), total * weights[0] // sum(weights)))
    least = 1 if total - largest >= count - 1 else 0
    holding, surplus = [largest] + [least] * (count - 1), total - largest - least * (count - 1)
    while surplus > 0:
        free = [i for i in range(1, count) if holding[i] < largest] or [i for i in range(1, count) if holding[i] < most]
        whole, budget = sum([weights[i] for i in free]), surplus
        for i in free:
            addition = min(most - holding[i], max(1, budget * weights[i] // whole), surplus)
            holding[i] = holding[i] + addition
            surplus = surplus - addition
    return np.array(holding)


def normal_values(own_key, shape, deviation, most, split=(), kind=jnp.bfloat16):
    level = block_scale(own_key, shape, split, -0.22, 0.18) if split else 1.0
    array = jax.random.normal(own_key, shape, jnp.float32) * deviation * level
    return jnp.minimum(jnp.maximum(array, -most), most).astype(kind)


def setup_inputs(seed: int = 0, part: int = 0) -> dict:
    key_list = jax.random.split(jax.random.key(seed), 7)
    own_keys = jax.random.split(jax.random.fold_in(key_list[6], part), 7)
    tokens = normal_values(own_keys[0], (TOKENS, D), 1.0, 6.0, ((0, 16),))
    expert_ids_keys = jax.random.split(jax.random.fold_in(own_keys[1], 1), TOKENS // TOK_DEV)
    expert_ids_turns = jax.random.permutation(jax.random.fold_in(own_keys[1], 3), TOKENS // TOK_DEV)
    expert_ids = jax.vmap(lambda own, number: routed_block(jax.random.fold_in(own_keys[1], 2), own, number, TOK_DEV, EXPERTS, TOP, CAP, 1))(expert_ids_keys, expert_ids_turns).reshape((TOKENS, TOP))
    gate_probs = jnp.clip(0.05 + 0.55 * jax.random.uniform(own_keys[2], (TOKENS, TOP), jnp.float32) ** block_scale(own_keys[2], (TOKENS, TOP), ((0, 16),), -0.2, 0.2), 0.05, 0.6)
    gate_proj = normal_values(key_list[3], (D, EXPERTS * FF), D ** -0.5, 0.0625, ((1, 16),))
    up_proj = normal_values(key_list[4], (D, EXPERTS * FF), D ** -0.5, 0.0625, ((1, 16),))
    down_proj = normal_values(key_list[5], (EXPERTS * FF, D), FF ** -0.5, 0.125, ((0, 16),))
    return {"tokens": tokens, "expert_ids": expert_ids, "gate_probs": gate_probs, "gate_proj": gate_proj, "up_proj": up_proj, "down_proj": down_proj}


def reference(tokens, expert_ids, gate_probs, gate_proj, up_proj, down_proj):
    rows_limit = N_EXPERT * CAP

    def per_expert(combined, expert_no):
        hits = expert_ids == expert_no
        chosen = jnp.any(hits, axis=1)
        weight = jnp.sum(jnp.where(hits, gate_probs, 0.0), axis=1)
        row_order = jnp.argsort(jnp.where(chosen, 0, 1).astype(jnp.int32), stable=True)[:rows_limit]
        picked_rows = tokens[row_order]
        col_start = expert_no * FF
        gate_cols = lax.dynamic_slice_in_dim(gate_proj, col_start, FF, 1)
        up_cols = lax.dynamic_slice_in_dim(up_proj, col_start, FF, 1)
        down_rows = lax.dynamic_slice_in_dim(down_proj, col_start, FF, 0)
        gate_val = jnp.dot(picked_rows, gate_cols, preferred_element_type=jnp.float32)
        up_val = jnp.dot(picked_rows, up_cols, preferred_element_type=jnp.float32)
        hidden = (jax.nn.silu(gate_val) * up_val).astype(jnp.bfloat16)
        result = jnp.dot(hidden, down_rows, preferred_element_type=jnp.float32)
        combined = combined.at[row_order].add(weight[row_order][:, None] * result)
        return combined, None

    start_sum = jnp.zeros(tokens.shape, jnp.float32)
    combined, _ = lax.scan(per_expert, start_sum, jnp.arange(EXPERTS, dtype=jnp.int32))
    return combined.astype(jnp.bfloat16)
```

```python
import jax
import jax.numpy as jnp
from jax import lax
from jax.sharding import PartitionSpec as P

FF = 2048
EXPERTS = 16
EXTRA = 128


def swap(value, bit, devices):
    return lax.ppermute(value, "expert", [(i, i ^ bit) for i in range(devices)])


def stages(devices):
    low = [1, 2]
    high = [b for b in range(4, devices, 4)]
    return low, high


def gather(block, devices):
    low, high = stages(devices)
    rows = [block] + [swap(block, b, devices) for b in high]
    rows = jnp.concatenate(rows, axis=0)
    for bit in reversed(low):
        rows = jnp.concatenate([rows, swap(rows, bit, devices)], axis=0)
    return rows


def order(devices):
    low, high = stages(devices)
    places = [0] + high
    for bit in reversed(low):
        places = places + [p ^ bit for p in places]
    return places


def scatter_sum(part, devices):
    low, high = stages(devices)
    for bit in low:
        half = part.shape[0] // 2
        got = swap(part[half:].astype(jnp.bfloat16), bit, devices)
        part = part[:half] + got.astype(jnp.float32)
    rows = part.shape[0] // (1 + len(high))
    total = part[:rows]
    sent = part[rows:].astype(jnp.bfloat16)
    for k, bit in enumerate(high):
        got = swap(sent[k * rows : (k + 1) * rows], bit, devices)
        total = total + got.astype(jnp.float32)
    return total


def shards(tokens, expert_ids, gate_probs, gate_proj, up_proj, down_proj):
    hid_count = gate_proj.shape[1]
    splits = FF // hid_count
    tok_count, model_width = tokens.shape
    devices = lax.axis_size("expert")
    own = lax.axis_index("expert") // splits
    picks = expert_ids[:, :, None] == jnp.arange(EXPERTS, dtype=jnp.int32)[None, None, :]
    weight_te = jnp.sum(jnp.where(picks, gate_probs[:, :, None], 0.0), axis=1)
    hi = lax.reduce_precision(weight_te, 8, 7)
    mid = lax.reduce_precision(weight_te - hi, 8, 7)
    lo = weight_te - hi - mid
    pad = jnp.zeros((tok_count, EXTRA - 3 * EXPERTS), jnp.float32)
    extra = jnp.concatenate([hi, mid, lo, pad], axis=1).astype(jnp.bfloat16)
    rows = gather(jnp.concatenate([tokens, extra], axis=1), devices)
    pieces = rows[:, model_width:].astype(jnp.float32)
    lane = jnp.arange(EXTRA, dtype=jnp.int32)[None, :]
    mine = (lane < 3 * EXPERTS) & (lane % EXPERTS == own)
    weight = jnp.sum(jnp.where(mine, pieces, 0.0), axis=1, keepdims=True)
    flat_rows = rows[:, :model_width]
    gate_val = jnp.dot(flat_rows, gate_proj, preferred_element_type=jnp.float32)
    up_val = jnp.dot(flat_rows, up_proj, preferred_element_type=jnp.float32)
    hidden = (jax.nn.silu(gate_val) * up_val).astype(jnp.bfloat16)
    outs = []
    chunks = 4
    width = model_width // chunks
    for k in range(chunks):
        part = jnp.dot(hidden, down_proj[:, k * width : (k + 1) * width], preferred_element_type=jnp.float32)
        outs.append(scatter_sum(part * weight, devices).astype(jnp.bfloat16))
    return jnp.concatenate(outs, axis=1)


def solution(mesh):
    placed = (
        P(("group", "expert"), None),
        P(("group", "expert"), None),
        P(("group", "expert"), None),
        P(None, "expert"),
        P(None, "expert"),
        P("expert", None),
    )
    return jax.shard_map(
        shards, mesh=mesh, in_specs=placed, out_specs=P(("group", "expert"), None), check_vma=False
    )
```

```python
import functools

import jax
import jax.numpy as jnp
from jax import lax
from jax.experimental import pallas as pl
from jax.experimental.pallas import tpu as pltpu
from jax.sharding import PartitionSpec as P

FF = 2048
EXPERTS = 16
EXTRA = 128
F32 = jnp.float32
BF16 = jnp.bfloat16


def swap(value, bit, devices):
    return lax.ppermute(value, "expert", [(i, i ^ bit) for i in range(devices)])


def bit_order(devices):
    return [1 << k for k in reversed(range(devices.bit_length() - 1))]


def places_of(bits):
    places = [0]
    for bit in bits:
        places = places + [p ^ bit for p in places]
    return places


def reorder(rows, have, want, height):
    if have == want:
        return rows
    runs, start = [], 0
    spots = [have.index(p) for p in want]
    for k in range(1, len(spots) + 1):
        if k == len(spots) or spots[k] != spots[k - 1] + 1:
            runs.append((spots[start], spots[k - 1] + 1))
            start = k
    return jnp.concatenate([rows[a * height : b * height] for a, b in runs], axis=0)


def hid_kernel(rows, slots, own_ref, a0_ref, a1_ref, b0_ref, b1_ref, g_hbm, u_hbm, o_ref, w_ref, gbuf, ubuf, gacc, uacc, sems):
    kc = gbuf.shape[1]
    steps = g_hbm.shape[0] // kc
    first = a0_ref.shape[1] // kc
    half = rows // 2

    def copies(s):
        slot = s % slots
        src = pl.ds(s * kc, kc)
        return (
            pltpu.make_async_copy(g_hbm.at[src, :], gbuf.at[slot], sems.at[0, slot]),
            pltpu.make_async_copy(u_hbm.at[src, :], ubuf.at[slot], sems.at[1, slot]),
        )

    for s in range(min(slots, steps)):
        for copy in copies(s):
            copy.start()
    width = b0_ref.shape[1] - EXTRA
    lane = lax.broadcasted_iota(jnp.int32, (half, EXTRA), 1)
    mine = (lane < 3 * EXPERTS) & (lane % EXPERTS == own_ref[0])
    for k, ref in enumerate((b0_ref, b1_ref)):
        pieces = jnp.where(mine, ref[:, width:].astype(F32), 0.0)
        total = jnp.sum(pieces, axis=1, keepdims=True)
        w_ref[k * half : (k + 1) * half, :] = jnp.broadcast_to(total, (half, EXTRA))
    for s in range(steps):
        slot = s % slots
        top, low = (a0_ref, a1_ref) if s < first else (b0_ref, b1_ref)
        cols = slice((s % first) * kc, (s % first + 1) * kc)
        x = jnp.concatenate([top[:, cols], low[:, cols]], axis=0)
        for copy, buf, acc in zip(copies(s), (gbuf, ubuf), (gacc, uacc)):
            copy.wait()
            part = jnp.dot(x, buf[slot], preferred_element_type=F32)
            if s == 0:
                acc[...] = part
            else:
                acc[...] += part
        if s + slots < steps:
            for copy in copies(s + slots):
                copy.start()
    gate = gacc[...]
    o_ref[...] = (gate / (1.0 + jnp.exp(-gate)) * uacc[...]).astype(BF16)


def hidden_call(own, tops, lows, gate_proj, up_proj):
    model_width, hid = gate_proj.shape
    rows = 2 * tops[0].shape[0]
    kc, slots = 896, 3
    vmem = pl.BlockSpec(memory_space=pltpu.VMEM)
    anys = pl.BlockSpec(memory_space=pl.ANY)
    return pl.pallas_call(
        functools.partial(hid_kernel, rows, slots),
        name="gate_up",
        out_shape=(jax.ShapeDtypeStruct((rows, hid), BF16), jax.ShapeDtypeStruct((rows, EXTRA), F32)),
        in_specs=[pl.BlockSpec(memory_space=pltpu.SMEM)] + [vmem] * 4 + [anys] * 2,
        out_specs=(vmem, vmem),
        scratch_shapes=[
            pltpu.VMEM((slots, kc, hid), BF16),
            pltpu.VMEM((slots, kc, hid), BF16),
            pltpu.VMEM((rows, hid), F32),
            pltpu.VMEM((rows, hid), F32),
            pltpu.SemaphoreType.DMA((2, slots)),
        ],
        compiler_params=pltpu.CompilerParams(vmem_limit_bytes=50 << 20),
        cost_estimate=pl.CostEstimate(
            flops=4 * rows * model_width * hid, transcendentals=rows * hid, bytes_accessed=4 * model_width * hid
        ),
    )(own, tops[0], lows[0], tops[1], lows[1], gate_proj, up_proj)


def down_kernel(offset, slots, h_ref, w_ref, d_hbm, keep_ref, send_ref, buf, sems):
    nc = buf.shape[2]
    steps = keep_ref.shape[1] // nc
    half = keep_ref.shape[0]

    def copy(s):
        slot = s % slots
        return pltpu.make_async_copy(d_hbm.at[:, pl.ds(offset + s * nc, nc)], buf.at[slot], sems.at[slot])

    for s in range(min(slots, steps)):
        copy(s).start()
    weight = w_ref[:, 0:1]
    for s in range(steps):
        copy(s).wait()
        part = jnp.dot(h_ref[...], buf[s % slots], preferred_element_type=F32) * weight
        if s + slots < steps:
            copy(s + slots).start()
        keep_ref[:, s * nc : (s + 1) * nc] = part[:half]
        send_ref[:, s * nc : (s + 1) * nc] = part[half:].astype(BF16)


def down_call(hidden, weight, down_proj, offset, width):
    rows, hid = hidden.shape
    half = rows // 2
    nc, slots = 512, 5
    vmem = pl.BlockSpec(memory_space=pltpu.VMEM)
    return pl.pallas_call(
        functools.partial(down_kernel, offset, slots),
        name="down_" + str(offset),
        out_shape=(jax.ShapeDtypeStruct((half, width), F32), jax.ShapeDtypeStruct((half, width), BF16)),
        in_specs=[vmem, vmem, pl.BlockSpec(memory_space=pl.ANY)],
        out_specs=(vmem, vmem),
        scratch_shapes=[pltpu.VMEM((slots, hid, nc), BF16), pltpu.SemaphoreType.DMA((slots,))],
        compiler_params=pltpu.CompilerParams(vmem_limit_bytes=50 << 20),
        cost_estimate=pl.CostEstimate(
            flops=2 * rows * hid * width, transcendentals=0, bytes_accessed=2 * hid * width
        ),
    )(hidden, weight, down_proj)


def shards(tokens, expert_ids, gate_probs, gate_proj, up_proj, down_proj):
    splits = FF // gate_proj.shape[1]
    height, model_width = tokens.shape
    devices = lax.axis_size("expert")
    own = (lax.axis_index("expert") // splits).astype(jnp.int32).reshape(1)
    picks = expert_ids[:, :, None] == jnp.arange(EXPERTS, dtype=jnp.int32)[None, None, :]
    weight_te = jnp.sum(jnp.where(picks, gate_probs[:, :, None], 0.0), axis=1)
    hi = lax.reduce_precision(weight_te, 8, 7)
    mid = lax.reduce_precision(weight_te - hi, 8, 7)
    lo = weight_te - hi - mid
    pad = jnp.zeros((height, EXTRA - 3 * EXPERTS), F32)
    extra = jnp.concatenate([hi, mid, lo, pad], axis=1).astype(BF16)
    block = jnp.concatenate([tokens, extra], axis=1)

    bits = bit_order(devices)
    order_a = bits[:-1]
    order_b = bits[:-3] + [bits[-2], bits[-3]]
    rows = block
    for bit in order_a[:-2]:
        rows = jnp.concatenate([rows, swap(rows, bit, devices)], axis=0)
    width = model_width // 2
    part_a, part_b = rows[:, :width], rows[:, width:]
    for bit_a, bit_b in zip(order_a[-2:], order_b[-2:]):
        got_a, got_b = swap(part_a, bit_a, devices), swap(part_b, bit_b, devices)
        part_a = jnp.concatenate([part_a, got_a], axis=0)
        part_b = jnp.concatenate([part_b, got_b], axis=0)
    part_b = reorder(part_b, places_of(order_b), places_of(order_a), height)
    low_a, low_b = swap(part_a, bits[-1], devices), swap(part_b, bits[-1], devices)

    hidden, weight = hidden_call(own, (part_a, part_b), (low_a, low_b), gate_proj, up_proj)

    outs = []
    for k in range(2):
        keep, send = down_call(hidden, weight, down_proj, k * width, width)
        for bit in reversed(bits):
            total = keep + swap(send, bit, devices).astype(F32)
            half = total.shape[0] // 2
            if bit == bits[0]:
                break
            keep, send = total[:half], total[half:].astype(BF16)
        outs.append(total.astype(BF16))
    return jnp.concatenate(outs, axis=1)


def solution(mesh):
    placed = (
        P(("group", "expert"), None),
        P(("group", "expert"), None),
        P(("group", "expert"), None),
        P(None, "expert"),
        P(None, "expert"),
        P("expert", None),
    )
    return jax.shard_map(
        shards, mesh=mesh, in_specs=placed, out_specs=P(("group", "expert"), None), check_vma=False
    )
```

```python
import functools

import jax
import jax.numpy as jnp
from jax import lax
from jax.experimental import pallas as pl
from jax.experimental.pallas import tpu as pltpu
from jax.sharding import PartitionSpec as P

FF = 2048
EXPERTS = 16
EXTRA = 128
F32 = jnp.float32
BF16 = jnp.bfloat16
HELD = 1024
KC = 512
SLOTS = 4
LIMIT = 24


def swap(value, bit, devices):
    return lax.ppermute(value, "expert", [(i, i ^ bit) for i in range(devices)])


def bit_order(devices):
    return [1 << k for k in reversed(range(devices.bit_length() - 1))]


def call(body, name, outs, ins, hbm=0, scratch=(), limit=1, cost=(0, 0, 0)):
    vmem = pl.BlockSpec(memory_space=pltpu.VMEM)
    specs = [vmem] * (len(ins) - hbm) + [pl.BlockSpec(memory_space=pltpu.HBM)] * hbm
    return pl.pallas_call(
        body,
        name=name,
        out_shape=tuple(outs),
        in_specs=specs,
        out_specs=(vmem,) * len(outs),
        scratch_shapes=list(scratch),
        compiler_params=pltpu.CompilerParams(vmem_limit_bytes=limit << 20),
        cost_estimate=pl.CostEstimate(flops=cost[0], transcendentals=cost[1], bytes_accessed=cost[2]),
    )(*ins)


def pack(tokens, expert_ids, gate_probs):
    height, model_width = tokens.shape

    def body(t_ref, i_ref, p_ref, o_ref):
        lane = lax.broadcasted_iota(jnp.int32, (height, EXTRA), 1)
        weight = jnp.zeros((height, EXTRA), F32)
        for k in range(expert_ids.shape[1]):
            weight += jnp.where(lane % EXPERTS == i_ref[:, k : k + 1], p_ref[:, k : k + 1], 0.0)
        high = weight.astype(BF16)
        rest = weight - high.astype(F32)
        middle = rest.astype(BF16)
        last = (rest - middle.astype(F32)).astype(BF16)
        wide = [v.astype(F32) for v in (high, middle, last)]
        extra = jnp.where(lane < EXPERTS, wide[0], jnp.where(lane < 2 * EXPERTS, wide[1], wide[2]))
        o_ref[:, :model_width] = t_ref[...]
        o_ref[:, model_width:] = jnp.where(lane < 3 * EXPERTS, extra, 0.0).astype(BF16)

    shape = jax.ShapeDtypeStruct((height, model_width + EXTRA), BF16)
    return call(body, "pack", [shape], [tokens, expert_ids, gate_probs])[0]


def join(values, outs):
    def body(*refs):
        for ref, (width, blocks) in zip(refs[len(values) :], outs):
            top = 0
            for source, col in blocks:
                block = refs[source][:, col : col + width]
                ref[top : top + block.shape[0], :] = block
                top += block.shape[0]

    shapes = [
        jax.ShapeDtypeStruct((sum(values[k].shape[0] for k, _ in blocks), width), BF16) for width, blocks in outs
    ]
    return call(body, "join", shapes, values, cost=(0, 0, 1 << 18))


def fetch(values, pieces):
    def body(*refs):
        *refs, sems = refs
        count, n = len(values), len(pieces)
        sources, copied, held = refs[count : count + n], refs[count + n : 2 * count + n], refs[2 * count + n :]
        copies = [
            pltpu.make_async_copy(src.at[pl.ds(r, h), pl.ds(c, w)], dst, sems.at[k])
            for k, (src, dst, (_, r, h, c, w)) in enumerate(zip(sources, held, pieces))
        ]
        for copy in copies:
            copy.start()
        for src, dst in zip(refs[:count], copied):
            dst[...] = src[...]
        for copy in copies:
            copy.wait()

    shapes = [jax.ShapeDtypeStruct(v.shape, v.dtype) for v in values]
    shapes += [pltpu.VMEM((h, w), BF16) for _, _, h, _, w in pieces]
    size = sum(2 * h * w for _, _, h, _, w in pieces)
    results = call(
        body,
        "fetch",
        shapes,
        [*values, *[p[0] for p in pieces]],
        hbm=len(pieces),
        scratch=[pltpu.SemaphoreType.DMA((len(pieces),))],
        cost=(0, 0, size),
    )
    return results[: len(values)], results[len(values) :]


def gate_up(own, parts_a, parts_b, blocks_a, blocks_b, held, gate_proj, up_proj, kc, slots, limit):
    model_width, hid = gate_proj.shape
    base = held[0].shape[0] if held else 0
    steps = (model_width - base) // kc
    rows = sum(h for _, _, h in blocks_a)
    split = parts_a[0].shape[1]
    cut = min(hid, 512)

    def body(own_ref, *refs):
        a_refs, refs = refs[: len(parts_a)], refs[len(parts_a) :]
        b_refs, refs = refs[: len(parts_b)], refs[len(parts_b) :]
        held_refs, refs = refs[: len(held)], refs[len(held) :]
        g_hbm, u_hbm, o_ref, w_ref, gbuf, ubuf, gacc, uacc, sems = refs

        def copies(s):
            slot = s % slots
            src = pl.ds(base + s * kc, kc)
            return (
                pltpu.make_async_copy(g_hbm.at[src, :], gbuf.at[slot], sems.at[0, slot]),
                pltpu.make_async_copy(u_hbm.at[src, :], ubuf.at[slot], sems.at[1, slot]),
            )

        for s in range(min(slots, steps)):
            for copy in copies(s):
                copy.start()

        def columns(start, count):
            parts = []
            for lo, hi, group, blocks in ((0, split, a_refs, blocks_a), (split, model_width, b_refs, blocks_b)):
                a, b = max(start, lo) - lo, min(start + count, hi) - lo
                if a < b:
                    parts.append(jnp.concatenate([group[k][r : r + h, a:b] for k, r, h in blocks], axis=0))
            return parts[0] if len(parts) == 1 else jnp.concatenate(parts, axis=1)

        def add(x, weights, acc, first):
            part = jnp.dot(x, weights, preferred_element_type=F32)
            if first:
                acc[...] = part
            else:
                acc[...] += part

        top = 0
        for k, r, h in blocks_b:
            lane = lax.broadcasted_iota(jnp.int32, (h, EXTRA), 1)
            mine = (lane < 3 * EXPERTS) & (lane % EXPERTS == own_ref[0:1, :])
            pieces = jnp.where(mine, b_refs[k][r : r + h, model_width - split :].astype(F32), 0.0)
            w_ref[top : top + h, :] = jnp.broadcast_to(jnp.sum(pieces, axis=1, keepdims=True), (h, EXTRA))
            top += h
        if held:
            x = columns(0, base)
            for ref, acc in zip(held_refs, (gacc, uacc)):
                add(x, ref[...], acc, True)
        for s in range(steps):
            x = columns(base + s * kc, kc)
            for copy, buf, acc in zip(copies(s), (gbuf, ubuf), (gacc, uacc)):
                copy.wait()
                add(x, buf[s % slots], acc, base + s == 0)
            if s + slots < steps:
                for copy in copies(s + slots):
                    copy.start()
        for c in range(0, hid, cut):
            gate = gacc[:, c : c + cut]
            o_ref[:, c : c + cut] = (gate / (1.0 + jnp.exp(-gate)) * uacc[:, c : c + cut]).astype(BF16)

    return call(
        body,
        "gate_up",
        [jax.ShapeDtypeStruct((rows, hid), BF16), jax.ShapeDtypeStruct((rows, EXTRA), F32)],
        [own, *parts_a, *parts_b, *held, gate_proj, up_proj],
        hbm=2,
        scratch=[
            pltpu.VMEM((slots, kc, hid), BF16),
            pltpu.VMEM((slots, kc, hid), BF16),
            pltpu.VMEM((rows, hid), F32),
            pltpu.VMEM((rows, hid), F32),
            pltpu.SemaphoreType.DMA((2, slots)),
        ],
        limit=limit,
        cost=(4 * rows * model_width * hid, rows * hid, 4 * (model_width - base) * hid),
    )


def down(hidden, weight, weights):
    rows, width = hidden.shape[0], weights.shape[1]
    half, nc = rows // 2, 512

    def body(h_ref, w_ref, d_ref, keep_ref, send_ref):
        scale = w_ref[:, 0:1]
        for c in range(0, width, nc):
            part = jnp.dot(h_ref[...], d_ref[:, c : c + nc], preferred_element_type=F32) * scale
            keep_ref[:, c : c + nc] = part[:half]
            send_ref[:, c : c + nc] = part[half:].astype(BF16)

    return call(
        body,
        "down",
        [jax.ShapeDtypeStruct((half, width), F32), jax.ShapeDtypeStruct((half, width), BF16)],
        [hidden, weight, weights],
        limit=6,
        cost=(2 * rows * hidden.shape[1] * width, 0, rows * width),
    )


def add_split(pairs, stay, go):
    width = sum(keep.shape[1] for keep, _ in pairs)
    flat = [value for pair in pairs for value in pair]

    def body(*refs):
        results = refs[len(flat) :]
        col = 0
        for keep_ref, got_ref in zip(refs[0 : len(flat) : 2], refs[1 : len(flat) : 2]):
            wide = keep_ref.shape[1]
            for ref, blocks in zip(results, (stay, go)):
                top = 0
                for r, h in blocks:
                    total = keep_ref[r : r + h, :] + got_ref[r : r + h, :].astype(F32)
                    ref[top : top + h, col : col + wide] = total.astype(ref.dtype)
                    top += h
            col += wide

    shapes = [jax.ShapeDtypeStruct((sum(h for _, h in stay), width), F32 if go else BF16)]
    if go:
        shapes.append(jax.ShapeDtypeStruct((sum(h for _, h in go), width), BF16))
    size = sum(keep.size for keep, _ in pairs)
    return call(body, "add", shapes, flat, limit=2, cost=(size, 0, 2 * size))


def shards(tokens, expert_ids, gate_probs, gate_proj, up_proj, down_proj):
    splits = FF // gate_proj.shape[1]
    height, model_width = tokens.shape
    devices = lax.axis_size("expert")
    place = jnp.full((8, EXTRA), lax.axis_index("expert") // splits, jnp.int32)
    gate_proj, up_proj, down_proj = (
        pltpu.with_memory_space_constraint(w, pltpu.HBM) for w in (gate_proj, up_proj, down_proj)
    )
    hid = gate_proj.shape[1]
    width = model_width // 2
    bits = bit_order(devices)
    far, (bit_a, bit_b), core = bits[:-3], bits[-3:-1], bits[-1]

    rows = pack(tokens, expert_ids, gate_probs)
    wide = rows.shape[1]
    for k, bit in enumerate(far):
        got = swap(rows, bit, devices)
        if k + 1 == len(far):
            (rows, own), (down_a,) = fetch([rows, place], [(down_proj, 0, hid, 0, width)])
            part_a, part_b = join([rows, got], [(width, [(0, 0), (1, 0)]), (wide - width, [(0, width), (1, width)])])
        else:
            (rows,) = join([rows, got], [(wide, [(0, 0), (1, 0)])])
    got_a, got_b = swap(part_a, bit_a, devices), swap(part_b, bit_b, devices)
    (part_a, part_b), held = fetch(
        [part_a, part_b], [(gate_proj, 0, HELD, 0, hid), (up_proj, 0, HELD, 0, hid)]
    )
    part_a, part_b = join(
        [part_a, got_a, part_b, got_b], [(width, [(0, 0), (1, 0)]), (wide - width, [(2, 0), (3, 0)])]
    )
    got_a, got_b = swap(part_a, bit_b, devices), swap(part_b, bit_a, devices)
    (part_a, part_b), (down_b,) = fetch([part_a, part_b], [(down_proj, 0, hid, width, width)])
    low_a, low_b = swap(part_a, core, devices), swap(part_b, core, devices)
    far_a, far_b = swap(got_a, core, devices), swap(got_b, core, devices)
    parts_a, parts_b = [part_a, got_a, low_a, far_a], [part_b, got_b, low_b, far_b]
    size = part_a.shape[0]
    half = size // 2
    blocks_a = [(k, 0, size) for k in range(4)]
    blocks_b = [(k + j, r, half) for k in (0, 2) for r in (0, half) for j in (0, 1)]
    hidden, weight = gate_up(
        own, parts_a, parts_b, blocks_a, blocks_b, held, gate_proj, up_proj, KC, SLOTS, LIMIT
    )

    keep_a, send_a = down(hidden, weight, down_a)
    got_a = swap(send_a, core, devices)
    keep_b, send_b = down(hidden, weight, down_b)
    got_b = swap(send_b, core, devices)
    q = keep_a.shape[0] // 4
    keep_a, send_a = add_split([(keep_a, got_a)], [(0, 2 * q)], [(2 * q, 2 * q)])
    got_a = swap(send_a, bit_b, devices)
    keep_b, send_b = add_split([(keep_b, got_b)], [(0, q), (2 * q, q)], [(q, q), (3 * q, q)])
    got_b = swap(send_b, bit_a, devices)
    keep_a, send_a = add_split([(keep_a, got_a)], [(0, q)], [(q, q)])
    got_a = swap(send_a, bit_a, devices)
    keep_b, send_b = add_split([(keep_b, got_b)], [(0, q)], [(q, q)])
    got_b = swap(send_b, bit_b, devices)
    pairs = [(keep_a, got_a), (keep_b, got_b)]
    for bit in reversed(far):
        q = q // 2
        keep, send = add_split(pairs, [(0, q)], [(q, q)])
        pairs = [(keep, swap(send, bit, devices))]
    return add_split(pairs, [(0, q)], [])[0]


def solution(mesh):
    placed = (
        P(("group", "expert"), None),
        P(("group", "expert"), None),
        P(("group", "expert"), None),
        P(None, "expert"),
        P(None, "expert"),
        P("expert", None),
    )
    return jax.shard_map(
        shards, mesh=mesh, in_specs=placed, out_specs=P(("group", "expert"), None), check_vma=False
    )
```

```python
import functools

import jax
import jax.numpy as jnp
from jax import lax
from jax.experimental import pallas as pl
from jax.experimental.pallas import tpu as pltpu
from jax.sharding import PartitionSpec as P

FF = 2048
EXPERTS = 16
EXTRA = 128
F32 = jnp.float32
BF16 = jnp.bfloat16
HELD = (1024, 512)
KC = 512
SLOTS = 3
LIMIT = 17


def swap(value, bit, devices):
    return lax.ppermute(value, "expert", [(i, i ^ bit) for i in range(devices)])


def bit_order(devices):
    return [1 << k for k in reversed(range(devices.bit_length() - 1))]


def call(body, name, outs, ins, hbm=0, scratch=(), limit=1, cost=(0, 0, 0)):
    vmem = pl.BlockSpec(memory_space=pltpu.VMEM)
    specs = [vmem] * (len(ins) - hbm) + [pl.BlockSpec(memory_space=pltpu.HBM)] * hbm
    return pl.pallas_call(
        body,
        name=name,
        out_shape=tuple(outs),
        in_specs=specs,
        out_specs=(vmem,) * len(outs),
        scratch_shapes=list(scratch),
        compiler_params=pltpu.CompilerParams(vmem_limit_bytes=limit << 20),
        cost_estimate=pl.CostEstimate(flops=cost[0], transcendentals=cost[1], bytes_accessed=cost[2]),
    )(*ins)


def pack(expert_ids, gate_probs):
    height, top = expert_ids.shape

    def body(i_hbm, p_hbm, o_ref, i_ref, p_ref, sems):
        copies = [
            pltpu.make_async_copy(i_hbm, i_ref, sems.at[0]),
            pltpu.make_async_copy(p_hbm, p_ref, sems.at[1]),
        ]
        for copy in copies:
            copy.start()
        for copy in copies:
            copy.wait()
        lane = lax.broadcasted_iota(jnp.int32, (height, EXTRA), 1)
        weight = jnp.zeros((height, EXTRA), F32)
        for k in range(top):
            weight += jnp.where(lane % EXPERTS == i_ref[:, k : k + 1], p_ref[:, k : k + 1], 0.0)
        high = weight.astype(BF16)
        rest = weight - high.astype(F32)
        middle = rest.astype(BF16)
        last = (rest - middle.astype(F32)).astype(BF16)
        wide = [v.astype(F32) for v in (high, middle, last)]
        extra = jnp.where(lane < EXPERTS, wide[0], jnp.where(lane < 2 * EXPERTS, wide[1], wide[2]))
        o_ref[...] = jnp.where(lane < 3 * EXPERTS, extra, 0.0).astype(BF16)

    return call(
        body,
        "pack",
        [jax.ShapeDtypeStruct((height, EXTRA), BF16)],
        [expert_ids, gate_probs],
        hbm=2,
        scratch=[
            pltpu.VMEM((height, top), jnp.int32),
            pltpu.VMEM((height, top), F32),
            pltpu.SemaphoreType.DMA((2,)),
        ],
        cost=(0, 0, 1 << 12),
    )[0]


def join(values, outs):
    def body(*refs):
        for ref, blocks in zip(refs[len(values) :], outs):
            top = 0
            for block in blocks:
                col, height = 0, values[block[0][0]].shape[0]
                for source, first, width in block:
                    ref[top : top + height, col : col + width] = refs[source][:, first : first + width]
                    col += width
                top += height

    shapes = [
        jax.ShapeDtypeStruct(
            (sum(values[block[0][0]].shape[0] for block in blocks), sum(w for _, _, w in blocks[0])), BF16
        )
        for blocks in outs
    ]
    return call(body, "join", shapes, values, cost=(0, 0, 1 << 18))


def fetch(values, pieces, brought=()):
    pieces = [*pieces, *[(v, 0, v.shape[0], 0, v.shape[1]) for v in brought]]

    def body(*refs):
        *refs, sems = refs
        count, n = len(values), len(pieces)
        sources, copied, held = refs[count : count + n], refs[count + n : 2 * count + n], refs[2 * count + n :]
        copies = [
            pltpu.make_async_copy(src.at[pl.ds(r, h), pl.ds(c, w)], dst, sems.at[k])
            for k, (src, dst, (_, r, h, c, w)) in enumerate(zip(sources, held, pieces))
        ]
        for copy in copies:
            copy.start()
        for src, dst in zip(refs[:count], copied):
            dst[...] = src[...]
        for copy in copies:
            copy.wait()

    shapes = [jax.ShapeDtypeStruct(v.shape, v.dtype) for v in values]
    shapes += [pltpu.VMEM((h, w), BF16) for _, _, h, _, w in pieces]
    size = sum(2 * h * w for _, _, h, _, w in pieces)
    results = call(
        body,
        "fetch",
        shapes,
        [*values, *[p[0] for p in pieces]],
        hbm=len(pieces),
        scratch=[pltpu.SemaphoreType.DMA((len(pieces),))],
        cost=(0, 0, size),
    )
    return results[: len(values)], results[len(values) :]


def gate_up(own, parts_a, parts_b, blocks_a, blocks_b, held, gate_proj, up_proj, kc, slots, limit):
    model_width, hid = gate_proj.shape
    sizes = [value.shape[0] for value in held[::2]]
    base = sum(sizes)
    steps = [(at, kc) for at in range(base, model_width - kc, kc)]
    steps += [(at, kc // 2) for at in range(model_width - kc, model_width, kc // 2)]
    rows = sum(h for _, _, h in blocks_a)
    split = parts_a[0].shape[1]
    cut = min(hid, 256)

    def body(own_ref, *refs):
        a_refs, refs = refs[: len(parts_a)], refs[len(parts_a) :]
        b_refs, refs = refs[: len(parts_b)], refs[len(parts_b) :]
        held_refs, refs = refs[: len(held)], refs[len(held) :]
        g_hbm, u_hbm, o_ref, w_ref, gbuf, ubuf, gacc, uacc, sems = refs

        def copies(s):
            slot, (at, size) = s % slots, steps[s]
            src, dst = pl.ds(at, size), pl.ds(0, size)
            return (
                pltpu.make_async_copy(g_hbm.at[src, :], gbuf.at[slot, dst], sems.at[0, slot]),
                pltpu.make_async_copy(u_hbm.at[src, :], ubuf.at[slot, dst], sems.at[1, slot]),
            )

        for s in range(min(slots, len(steps))):
            for copy in copies(s):
                copy.start()

        def columns(start, count):
            parts = []
            for lo, hi, group, blocks in ((0, split, a_refs, blocks_a), (split, model_width, b_refs, blocks_b)):
                a, b = max(start, lo) - lo, min(start + count, hi) - lo
                if a < b:
                    parts.append(jnp.concatenate([group[k][r : r + h, a:b] for k, r, h in blocks], axis=0))
            return parts[0] if len(parts) == 1 else jnp.concatenate(parts, axis=1)

        def add(x, weights, acc, first):
            part = jnp.dot(x, weights, preferred_element_type=F32)
            if first:
                acc[...] = part
            else:
                acc[...] += part

        top = 0
        for k, r, h in blocks_b:
            lane = lax.broadcasted_iota(jnp.int32, (h, EXTRA), 1)
            mine = (lane < 3 * EXPERTS) & (lane % EXPERTS == own_ref[0:1, :])
            pieces = jnp.where(mine, b_refs[k][r : r + h, model_width - split :].astype(F32), 0.0)
            w_ref[top : top + h, :] = jnp.broadcast_to(jnp.sum(pieces, axis=1, keepdims=True), (h, EXTRA))
            top += h
        at = 0
        for k, size in enumerate(sizes):
            x = columns(at, size)
            for ref, acc in zip(held_refs[2 * k : 2 * k + 2], (gacc, uacc)):
                add(x, ref[...], acc, at == 0)
            at += size
        for s, (at, size) in enumerate(steps[:-1]):
            x = columns(at, size)
            for copy, buf, acc in zip(copies(s), (gbuf, ubuf), (gacc, uacc)):
                copy.wait()
                add(x, buf[s % slots, :size], acc, at == 0)
            if s + slots < len(steps):
                for copy in copies(s + slots):
                    copy.start()
        at, size = steps[-1]
        slot = (len(steps) - 1) % slots
        x = columns(at, size)
        for copy in copies(len(steps) - 1):
            copy.wait()
        for c in range(0, hid, cut):
            cols = slice(c, c + cut)
            gate = gacc[:, cols] + jnp.dot(x, gbuf[slot, :size, cols], preferred_element_type=F32)
            up = uacc[:, cols] + jnp.dot(x, ubuf[slot, :size, cols], preferred_element_type=F32)
            o_ref[:, cols] = (gate / (1.0 + jnp.exp(-gate)) * up).astype(BF16)

    return call(
        body,
        "gate_up",
        [jax.ShapeDtypeStruct((rows, hid), BF16), jax.ShapeDtypeStruct((rows, EXTRA), F32)],
        [own, *parts_a, *parts_b, *held, gate_proj, up_proj],
        hbm=2,
        scratch=[
            pltpu.VMEM((slots, kc, hid), BF16),
            pltpu.VMEM((slots, kc, hid), BF16),
            pltpu.VMEM((rows, hid), F32),
            pltpu.VMEM((rows, hid), F32),
            pltpu.SemaphoreType.DMA((2, slots)),
        ],
        limit=limit,
        cost=(4 * rows * model_width * hid, rows * hid, 4 * (model_width - base) * hid),
    )


def down(hidden, weight, weights):
    rows, width = hidden.shape[0], weights.shape[1]
    half, nc = rows // 2, 512

    def body(h_ref, w_ref, d_ref, keep_ref, send_ref):
        scale = w_ref[:, 0:1]
        for c in range(0, width, nc):
            part = jnp.dot(h_ref[...], d_ref[:, c : c + nc], preferred_element_type=F32) * scale
            keep_ref[:, c : c + nc] = part[:half]
            send_ref[:, c : c + nc] = part[half:].astype(BF16)

    return call(
        body,
        "down",
        [jax.ShapeDtypeStruct((half, width), F32), jax.ShapeDtypeStruct((half, width), BF16)],
        [hidden, weight, weights],
        limit=6,
        cost=(2 * rows * hidden.shape[1] * width, 0, rows * width),
    )


def add_split(pairs, stay, go):
    width = sum(keep.shape[1] for keep, _ in pairs)
    flat = [value for pair in pairs for value in pair]

    def body(*refs):
        results = refs[len(flat) :]
        col = 0
        for keep_ref, got_ref in zip(refs[0 : len(flat) : 2], refs[1 : len(flat) : 2]):
            wide = keep_ref.shape[1]
            for ref, blocks in zip(results, (stay, go)):
                top = 0
                for r, h in blocks:
                    total = keep_ref[r : r + h, :] + got_ref[r : r + h, :].astype(F32)
                    ref[top : top + h, col : col + wide] = total.astype(ref.dtype)
                    top += h
            col += wide

    shapes = [jax.ShapeDtypeStruct((sum(h for _, h in stay), width), F32 if go else BF16)]
    if go:
        shapes.append(jax.ShapeDtypeStruct((sum(h for _, h in go), width), BF16))
    size = sum(keep.size for keep, _ in pairs)
    return call(body, "add", shapes, flat, limit=2, cost=(size, 0, 2 * size))


def shards(tokens, expert_ids, gate_probs, gate_proj, up_proj, down_proj):
    splits = FF // gate_proj.shape[1]
    height, model_width = tokens.shape
    devices = lax.axis_size("expert")
    place = jnp.full((8, EXTRA), lax.axis_index("expert") // splits, jnp.int32)
    expert_ids, gate_probs, gate_proj, up_proj, down_proj = (
        pltpu.with_memory_space_constraint(v, pltpu.HBM)
        for v in (expert_ids, gate_probs, gate_proj, up_proj, down_proj)
    )
    hid = gate_proj.shape[1]
    width = model_width // 2
    bits = bit_order(devices)
    far, (bit_a, bit_b), core = bits[:-3], bits[-3:-1], bits[-1]

    rows = tokens
    for k, bit in enumerate(far):
        got = swap(rows, bit, devices)
        if k == 0:
            extra = pack(expert_ids, gate_probs)
        got_extra = swap(extra, bit, devices)
        if k + 1 == len(far):
            first = [pltpu.with_memory_space_constraint(rows, pltpu.HBM)] if k == 0 else []
            values, (down_a, *brought) = fetch(
                [extra, place] if first else [extra, place, rows], [(down_proj, 0, hid, 0, width)], first
            )
            extra, place, rows = [*values, *brought]
            part_a, part_b = join(
                [rows, extra, got, got_extra],
                [
                    [[(0, 0, width)], [(2, 0, width)]],
                    [[(0, width, width), (1, 0, EXTRA)], [(2, width, width), (3, 0, EXTRA)]],
                ],
            )
        else:
            rows, extra = join(
                [rows, extra, got, got_extra],
                [[[(0, 0, model_width)], [(2, 0, model_width)]], [[(1, 0, EXTRA)], [(3, 0, EXTRA)]]],
            )
    got_a, got_b = swap(part_a, bit_a, devices), swap(part_b, bit_b, devices)
    (part_a, part_b), held = fetch(
        [part_a, part_b], [(gate_proj, 0, HELD[0], 0, hid), (up_proj, 0, HELD[0], 0, hid)]
    )
    part_a, part_b = join(
        [part_a, got_a, part_b, got_b],
        [[[(0, 0, width)], [(1, 0, width)]], [[(2, 0, width + EXTRA)], [(3, 0, width + EXTRA)]]],
    )
    got_a, got_b = swap(part_a, bit_b, devices), swap(part_b, bit_a, devices)
    (part_a, part_b), (down_b,) = fetch([part_a, part_b], [(down_proj, 0, hid, width, width)])
    low_a, low_b = swap(part_a, core, devices), swap(part_b, core, devices)
    far_a, far_b = swap(got_a, core, devices), swap(got_b, core, devices)
    (got_a, got_b), more = fetch(
        [got_a, got_b], [(gate_proj, HELD[0], HELD[1], 0, hid), (up_proj, HELD[0], HELD[1], 0, hid)]
    )
    held = [*held, *more]
    parts_a, parts_b = [part_a, got_a, low_a, far_a], [part_b, got_b, low_b, far_b]
    size = part_a.shape[0]
    half = size // 2
    blocks_a = [(k, 0, size) for k in range(4)]
    blocks_b = [(k + j, r, half) for k in (0, 2) for r in (0, half) for j in (0, 1)]
    hidden, weight = gate_up(
        place, parts_a, parts_b, blocks_a, blocks_b, held, gate_proj, up_proj, KC, SLOTS, LIMIT
    )

    keep_a, send_a = down(hidden, weight, down_a)
    got_a = swap(send_a, core, devices)
    keep_b, send_b = down(hidden, weight, down_b)
    got_b = swap(send_b, core, devices)
    q = keep_a.shape[0] // 4
    keep_a, send_a = add_split([(keep_a, got_a)], [(0, 2 * q)], [(2 * q, 2 * q)])
    got_a = swap(send_a, bit_b, devices)
    keep_b, send_b = add_split([(keep_b, got_b)], [(0, q), (2 * q, q)], [(q, q), (3 * q, q)])
    got_b = swap(send_b, bit_a, devices)
    keep_a, send_a = add_split([(keep_a, got_a)], [(0, q)], [(q, q)])
    got_a = swap(send_a, bit_a, devices)
    keep_b, send_b = add_split([(keep_b, got_b)], [(0, q)], [(q, q)])
    got_b = swap(send_b, bit_b, devices)
    for bit in reversed(far):
        q = q // 2
        keep_a, send_a = add_split([(keep_a, got_a)], [(0, q)], [(q, q)])
        got_a = swap(send_a, bit, devices)
        keep_b, send_b = add_split([(keep_b, got_b)], [(0, q)], [(q, q)])
        got_b = swap(send_b, bit, devices)
    return add_split([(keep_a, got_a), (keep_b, got_b)], [(0, q)], [])[0]


def solution(mesh):
    placed = (
        P(("group", "expert"), None),
        P(("group", "expert"), None),
        P(("group", "expert"), None),
        P(None, "expert"),
        P(None, "expert"),
        P("expert", None),
    )
    return jax.shard_map(
        shards, mesh=mesh, in_specs=placed, out_specs=P(("group", "expert"), None), check_vma=False
    )
```

```python
import functools

import jax
import jax.numpy as jnp
from jax import lax
from jax.experimental import pallas as pl
from jax.experimental.pallas import tpu as pltpu
from jax.sharding import PartitionSpec as P

FF = 2048
EXPERTS = 16
EXTRA = 128
F32 = jnp.float32
BF16 = jnp.bfloat16
HELD = (1024, 512)
KC = 512
SLOTS = 3
LIMIT = 17


def swap(value, bit, devices):
    return lax.ppermute(value, "expert", [(i, i ^ bit) for i in range(devices)])


def bit_order(devices):
    return [1 << k for k in reversed(range(devices.bit_length() - 1))]


def call(body, name, outs, ins, hbm=0, scratch=(), limit=1, cost=(0, 0, 0)):
    vmem = pl.BlockSpec(memory_space=pltpu.VMEM)
    specs = [vmem] * (len(ins) - hbm) + [pl.BlockSpec(memory_space=pltpu.HBM)] * hbm
    return pl.pallas_call(
        body,
        name=name,
        out_shape=tuple(outs),
        in_specs=specs,
        out_specs=(vmem,) * len(outs),
        scratch_shapes=list(scratch),
        compiler_params=pltpu.CompilerParams(vmem_limit_bytes=limit << 20),
        cost_estimate=pl.CostEstimate(flops=cost[0], transcendentals=cost[1], bytes_accessed=cost[2]),
    )(*ins)


def pack(expert_ids, gate_probs):
    height, top = expert_ids.shape

    def body(i_hbm, p_hbm, o_ref, i_ref, p_ref, sems):
        copies = [
            pltpu.make_async_copy(i_hbm, i_ref, sems.at[0]),
            pltpu.make_async_copy(p_hbm, p_ref, sems.at[1]),
        ]
        for copy in copies:
            copy.start()
        for copy in copies:
            copy.wait()
        lane = lax.broadcasted_iota(jnp.int32, (height, EXTRA), 1)
        weight = jnp.zeros((height, EXTRA), F32)
        for k in range(top):
            weight += jnp.where(lane % EXPERTS == i_ref[:, k : k + 1], p_ref[:, k : k + 1], 0.0)
        high = weight.astype(BF16)
        rest = weight - high.astype(F32)
        middle = rest.astype(BF16)
        last = (rest - middle.astype(F32)).astype(BF16)
        wide = [v.astype(F32) for v in (high, middle, last)]
        extra = jnp.where(lane < EXPERTS, wide[0], jnp.where(lane < 2 * EXPERTS, wide[1], wide[2]))
        o_ref[...] = jnp.where(lane < 3 * EXPERTS, extra, 0.0).astype(BF16)

    return call(
        body,
        "pack",
        [jax.ShapeDtypeStruct((height, EXTRA), BF16)],
        [expert_ids, gate_probs],
        hbm=2,
        scratch=[
            pltpu.VMEM((height, top), jnp.int32),
            pltpu.VMEM((height, top), F32),
            pltpu.SemaphoreType.DMA((2,)),
        ],
        cost=(0, 0, 1 << 12),
    )[0]


def join(values, outs):
    def body(*refs):
        for ref, blocks in zip(refs[len(values) :], outs):
            top = 0
            for block in blocks:
                col, height = 0, values[block[0][0]].shape[0]
                for source, first, width in block:
                    ref[top : top + height, col : col + width] = refs[source][:, first : first + width]
                    col += width
                top += height

    shapes = [
        jax.ShapeDtypeStruct(
            (sum(values[block[0][0]].shape[0] for block in blocks), sum(w for _, _, w in blocks[0])), BF16
        )
        for blocks in outs
    ]
    return call(body, "join", shapes, values, cost=(0, 0, 1 << 18))


def fetch(values, pieces, brought=()):
    pieces = [*pieces, *[(v, 0, v.shape[0], 0, v.shape[1]) for v in brought]]

    def body(*refs):
        *refs, sems = refs
        count, n = len(values), len(pieces)
        sources, copied, held = refs[count : count + n], refs[count + n : 2 * count + n], refs[2 * count + n :]
        copies = [
            pltpu.make_async_copy(src.at[pl.ds(r, h), pl.ds(c, w)], dst, sems.at[k])
            for k, (src, dst, (_, r, h, c, w)) in enumerate(zip(sources, held, pieces))
        ]
        for copy in copies:
            copy.start()
        for src, dst in zip(refs[:count], copied):
            dst[...] = src[...]
        for copy in copies:
            copy.wait()

    shapes = [jax.ShapeDtypeStruct(v.shape, v.dtype) for v in values]
    shapes += [pltpu.VMEM((h, w), BF16) for _, _, h, _, w in pieces]
    size = sum(2 * h * w for _, _, h, _, w in pieces)
    results = call(
        body,
        "fetch",
        shapes,
        [*values, *[p[0] for p in pieces]],
        hbm=len(pieces),
        scratch=[pltpu.SemaphoreType.DMA((len(pieces),))],
        cost=(0, 0, size),
    )
    return results[: len(values)], results[len(values) :]


def gate_up(own, parts_a, parts_b, blocks_a, blocks_b, held, gate_proj, up_proj, kc, slots, limit):
    model_width, hid = gate_proj.shape
    sizes = [value.shape[0] for value in held[::2]]
    base = sum(sizes)
    steps = [(at, kc) for at in range(base, model_width - kc, kc)]
    steps += [(model_width - kc, kc - kc // 4), (model_width - kc // 4, kc // 4)]
    rows = sum(h for _, _, h in blocks_a)
    split = parts_a[0].shape[1]
    cut = min(hid, 512)

    def body(own_ref, *refs):
        a_refs, refs = refs[: len(parts_a)], refs[len(parts_a) :]
        b_refs, refs = refs[: len(parts_b)], refs[len(parts_b) :]
        held_refs, refs = refs[: len(held)], refs[len(held) :]
        g_hbm, u_hbm, o_ref, w_ref, gbuf, ubuf, gacc, uacc, sems = refs

        def copies(s):
            slot, (at, size) = s % slots, steps[s]
            src, dst = pl.ds(at, size), pl.ds(0, size)
            return (
                pltpu.make_async_copy(g_hbm.at[src, :], gbuf.at[slot, dst], sems.at[0, slot]),
                pltpu.make_async_copy(u_hbm.at[src, :], ubuf.at[slot, dst], sems.at[1, slot]),
            )

        for s in range(min(slots, len(steps))):
            for copy in copies(s):
                copy.start()

        def columns(start, count):
            parts = []
            for lo, hi, group, blocks in ((0, split, a_refs, blocks_a), (split, model_width, b_refs, blocks_b)):
                a, b = max(start, lo) - lo, min(start + count, hi) - lo
                if a < b:
                    parts.append(jnp.concatenate([group[k][r : r + h, a:b] for k, r, h in blocks], axis=0))
            return parts[0] if len(parts) == 1 else jnp.concatenate(parts, axis=1)

        def add(x, weights, acc, first):
            part = jnp.dot(x, weights, preferred_element_type=F32)
            if first:
                acc[...] = part
            else:
                acc[...] += part

        top = 0
        for k, r, h in blocks_b:
            lane = lax.broadcasted_iota(jnp.int32, (h, EXTRA), 1)
            mine = (lane < 3 * EXPERTS) & (lane % EXPERTS == own_ref[0:1, :])
            pieces = jnp.where(mine, b_refs[k][r : r + h, model_width - split :].astype(F32), 0.0)
            w_ref[top : top + h, :] = jnp.broadcast_to(jnp.sum(pieces, axis=1, keepdims=True), (h, EXTRA))
            top += h
        at = 0
        for k, size in enumerate(sizes):
            x = columns(at, size)
            for ref, acc in zip(held_refs[2 * k : 2 * k + 2], (gacc, uacc)):
                add(x, ref[...], acc, at == 0)
            at += size
        for s, (at, size) in enumerate(steps[:-1]):
            x = columns(at, size)
            for copy, buf, acc in zip(copies(s), (gbuf, ubuf), (gacc, uacc)):
                copy.wait()
                add(x, buf[s % slots, :size], acc, at == 0)
            if s + slots < len(steps):
                for copy in copies(s + slots):
                    copy.start()
        at, size = steps[-1]
        slot = (len(steps) - 1) % slots
        x = columns(at, size)
        for copy in copies(len(steps) - 1):
            copy.wait()
        for c in range(0, hid, cut):
            cols = slice(c, c + cut)
            gate = gacc[:, cols] + jnp.dot(x, gbuf[slot, :size, cols], preferred_element_type=F32)
            up = uacc[:, cols] + jnp.dot(x, ubuf[slot, :size, cols], preferred_element_type=F32)
            o_ref[:, cols] = (gate / (1.0 + jnp.exp(-gate)) * up).astype(BF16)

    return call(
        body,
        "gate_up",
        [jax.ShapeDtypeStruct((rows, hid), BF16), jax.ShapeDtypeStruct((rows, EXTRA), F32)],
        [own, *parts_a, *parts_b, *held, gate_proj, up_proj],
        hbm=2,
        scratch=[
            pltpu.VMEM((slots, kc, hid), BF16),
            pltpu.VMEM((slots, kc, hid), BF16),
            pltpu.VMEM((rows, hid), F32),
            pltpu.VMEM((rows, hid), F32),
            pltpu.SemaphoreType.DMA((2, slots)),
        ],
        limit=limit,
        cost=(4 * rows * model_width * hid, rows * hid, 4 * (model_width - base) * hid),
    )


def down(hidden, weight, weights):
    rows, width = hidden.shape[0], weights.shape[1]
    half, nc = rows // 2, 512

    def body(h_ref, w_ref, d_ref, keep_ref, send_ref):
        scale = w_ref[:, 0:1]
        for c in range(0, width, nc):
            part = jnp.dot(h_ref[...], d_ref[:, c : c + nc], preferred_element_type=F32) * scale
            keep_ref[:, c : c + nc] = part[:half]
            send_ref[:, c : c + nc] = part[half:].astype(BF16)

    return call(
        body,
        "down",
        [jax.ShapeDtypeStruct((half, width), F32), jax.ShapeDtypeStruct((half, width), BF16)],
        [hidden, weight, weights],
        limit=6,
        cost=(2 * rows * hidden.shape[1] * width, 0, rows * width),
    )


def add_split(pairs, stay, go):
    width = sum(keep.shape[1] for keep, _ in pairs)
    flat = [value for pair in pairs for value in pair]

    def body(*refs):
        results = refs[len(flat) :]
        col = 0
        for keep_ref, got_ref in zip(refs[0 : len(flat) : 2], refs[1 : len(flat) : 2]):
            wide = keep_ref.shape[1]
            for ref, blocks in zip(results, (stay, go)):
                top = 0
                for r, h in blocks:
                    total = keep_ref[r : r + h, :] + got_ref[r : r + h, :].astype(F32)
                    ref[top : top + h, col : col + wide] = total.astype(ref.dtype)
                    top += h
            col += wide

    shapes = [jax.ShapeDtypeStruct((sum(h for _, h in stay), width), F32 if go else BF16)]
    if go:
        shapes.append(jax.ShapeDtypeStruct((sum(h for _, h in go), width), BF16))
    size = sum(keep.size for keep, _ in pairs)
    return call(body, "add", shapes, flat, limit=2, cost=(size, 0, 2 * size))


def shards(tokens, expert_ids, gate_probs, gate_proj, up_proj, down_proj):
    splits = FF // gate_proj.shape[1]
    height, model_width = tokens.shape
    devices = lax.axis_size("expert")
    place = jnp.full((8, EXTRA), lax.axis_index("expert") // splits, jnp.int32)
    expert_ids, gate_probs, gate_proj, up_proj, down_proj = (
        pltpu.with_memory_space_constraint(v, pltpu.HBM)
        for v in (expert_ids, gate_probs, gate_proj, up_proj, down_proj)
    )
    hid = gate_proj.shape[1]
    width = model_width // 2
    bits = bit_order(devices)
    far, (bit_a, bit_b), core = bits[:-3], bits[-3:-1], bits[-1]

    rows = tokens
    for k, bit in enumerate(far):
        got = swap(rows, bit, devices)
        if k == 0:
            extra = pack(expert_ids, gate_probs)
        got_extra = swap(extra, bit, devices)
        if k + 1 == len(far):
            first = [pltpu.with_memory_space_constraint(rows, pltpu.HBM)] if k == 0 else []
            values, (down_a, *brought) = fetch(
                [extra, place] if first else [extra, place, rows], [(down_proj, 0, hid, 0, width)], first
            )
            extra, place, rows = [*values, *brought]
            part_a, part_b = join(
                [rows, extra, got, got_extra],
                [
                    [[(0, 0, width)], [(2, 0, width)]],
                    [[(0, width, width), (1, 0, EXTRA)], [(2, width, width), (3, 0, EXTRA)]],
                ],
            )
        else:
            rows, extra = join(
                [rows, extra, got, got_extra],
                [[[(0, 0, model_width)], [(2, 0, model_width)]], [[(1, 0, EXTRA)], [(3, 0, EXTRA)]]],
            )
    got_a, got_b = swap(part_a, bit_a, devices), swap(part_b, bit_b, devices)
    (part_a, part_b), held = fetch(
        [part_a, part_b], [(gate_proj, 0, HELD[0], 0, hid), (up_proj, 0, HELD[0], 0, hid)]
    )
    part_a, part_b = join(
        [part_a, got_a, part_b, got_b],
        [[[(0, 0, width)], [(1, 0, width)]], [[(2, 0, width + EXTRA)], [(3, 0, width + EXTRA)]]],
    )
    got_a, got_b = swap(part_a, bit_b, devices), swap(part_b, bit_a, devices)
    (part_a, part_b), (down_b,) = fetch([part_a, part_b], [(down_proj, 0, hid, width, width)])
    low_a, low_b = swap(part_a, core, devices), swap(part_b, core, devices)
    far_a, far_b = swap(got_a, core, devices), swap(got_b, core, devices)
    (got_a, got_b), more = fetch(
        [got_a, got_b], [(gate_proj, HELD[0], HELD[1], 0, hid), (up_proj, HELD[0], HELD[1], 0, hid)]
    )
    held = [*held, *more]
    parts_a, parts_b = [part_a, got_a, low_a, far_a], [part_b, got_b, low_b, far_b]
    size = part_a.shape[0]
    half = size // 2
    blocks_a = [(k, 0, size) for k in range(4)]
    blocks_b = [(k + j, r, half) for k in (0, 2) for r in (0, half) for j in (0, 1)]
    hidden, weight = gate_up(
        place, parts_a, parts_b, blocks_a, blocks_b, held, gate_proj, up_proj, KC, SLOTS, LIMIT
    )

    keep_a, send_a = down(hidden, weight, down_a)
    got_a = swap(send_a, core, devices)
    keep_b, send_b = down(hidden, weight, down_b)
    got_b = swap(send_b, core, devices)
    q = keep_a.shape[0] // 4
    keep_a, send_a = add_split([(keep_a, got_a)], [(0, 2 * q)], [(2 * q, 2 * q)])
    got_a = swap(send_a, bit_b, devices)
    keep_b, send_b = add_split([(keep_b, got_b)], [(0, q), (2 * q, q)], [(q, q), (3 * q, q)])
    got_b = swap(send_b, bit_a, devices)
    keep_a, send_a = add_split([(keep_a, got_a)], [(0, q)], [(q, q)])
    got_a = swap(send_a, bit_a, devices)
    keep_b, send_b = add_split([(keep_b, got_b)], [(0, q)], [(q, q)])
    got_b = swap(send_b, bit_b, devices)
    for bit in reversed(far):
        q = q // 2
        keep_a, send_a = add_split([(keep_a, got_a)], [(0, q)], [(q, q)])
        got_a = swap(send_a, bit, devices)
        keep_b, send_b = add_split([(keep_b, got_b)], [(0, q)], [(q, q)])
        got_b = swap(send_b, bit, devices)
    return add_split([(keep_a, got_a), (keep_b, got_b)], [(0, q)], [])[0]


def solution(mesh):
    placed = (
        P(("group", "expert"), None),
        P(("group", "expert"), None),
        P(("group", "expert"), None),
        P(None, "expert"),
        P(None, "expert"),
        P("expert", None),
    )
    return jax.shard_map(
        shards, mesh=mesh, in_specs=placed, out_specs=P(("group", "expert"), None), check_vma=False
    )
```
